32 devices in a mesh: row: 4 (over y, x), col: 8 (over z, core).
Axes of the slice: x: 2, y: 2, z: 4, core: 2. Of those that a mesh axis runs over, the one named last changes fastest.
Arguments:
- pivot: float32 [1024, 1024], replicated, may hold values from -1 to 2
- col_panel: float32 [2048, 1024], P('row', 'col'), may hold values from -0.25 to 0.25
- row_panel: float32 [1024, 2048], P('row', 'col'), may hold values from -6 to 6
- trailing: float32 [2048, 2048], P('row', 'col'), may hold values from -6 to 6
Outputs:
- updated: float32 [2048, 2048], P('row', 'col')
The draws below stay inside these ranges and needn't reach their ends.
All inputs are finite; a program needn't handle non-finite values.
Results may differ from the reference program's by a relative error of at most 0.000061.
Values sent between devices are 32-bit elements; how exact they have to be, the bound alone decides.
No kernel may reach another device: no remote copies, remote signals or barrier semaphores. Data moves between devices by JAX's collectives and lax.ppermute only.
A program may use at most 64 MiB of HBM per device.

```python
import math
import jax
import jax.numpy as jnp
from jax import lax

B = 512
TRAIL_ROWS = 2048
TRAIL_COLS = 2048


def draw_pivot(key, part):
    noise = jax.random.normal(key, (2 * B, 2 * B), jnp.float32)
    return jnp.eye(2 * B, dtype=jnp.float32) + 0.25 / math.sqrt(B) * noise


def block_scale(own_key, extent, pieces, smallest, high):
    loudness, own = 1.0, jax.random.fold_in(own_key, 6)
    for dim, parts in pieces:
        heights = jnp.exp(jax.random.uniform(jax.random.fold_in(own, dim), (parts,), jnp.float32, smallest / len(pieces), high / len(pieces)))
        loudness = loudness * jnp.repeat(heights, extent[dim] // parts).reshape([-1 if axis == dim else 1 for axis in range(len(extent))])
    return loudness


def gaussian(rng, extent, deviation, bound, pieces=(), held_as=jnp.bfloat16):
    array = deviation * jax.random.normal(rng, extent, jnp.float32)
    if pieces:
        array = array * block_scale(rng, extent, pieces, -0.22, 0.18)
    return jnp.clip(array, -bound, bound).astype(held_as)


def setup_inputs(seed: int = 0) -> dict:
    keys = jax.random.split(jax.random.key(seed), 5)
    return {
        "pivot": draw_pivot(jax.random.fold_in(keys[4], 71), 0),
        "col_panel": gaussian(keys[1], (TRAIL_ROWS, 2 * B), B ** -0.5, 0.25, ((0, 4), (1, 8)), jnp.float32),
        "row_panel": gaussian(keys[2], (2 * B, TRAIL_COLS), 1.0, 6.0, ((0, 4), (1, 8)), jnp.float32),
        "trailing": gaussian(keys[3], (TRAIL_ROWS, TRAIL_COLS), 1.0, 6.0, ((0, 4), (1, 8)), jnp.float32),
    }


def product(left, right):
    return jnp.dot(left, right, precision=lax.Precision.HIGHEST, preferred_element_type=jnp.float32)


def newton_inverse(matrix):
    identity = jnp.eye(matrix.shape[0], dtype=jnp.float32)
    initial = 2.0 * identity - matrix
    return product(initial, 2.0 * identity - product(matrix, initial))


def reference(pivot, col_panel, row_panel, trailing):
    top_left = pivot[:B, :B]
    top_right = pivot[:B, B:]
    low_left = pivot[B:, :B]
    low_right = pivot[B:, B:]
    inverse_one = newton_inverse(top_left)
    multiplier = product(low_left, inverse_one)
    schur = low_right - product(multiplier, top_right)
    inverse_two = newton_inverse(schur)
    factor_one = product(col_panel[:, :B], inverse_one)
    factor_two = product(col_panel[:, B:] - product(factor_one, top_right), inverse_two)
    first_rows = row_panel[:B]
    rows_two = row_panel[B:] - product(multiplier, first_rows)
    return trailing - product(factor_one, first_rows) - product(factor_two, rows_two)
```

```python
import functools

import jax
import jax.numpy as jnp
from jax import lax
from jax.experimental import pallas as pl
from jax.experimental.pallas import tpu as pltpu
from jax.sharding import PartitionSpec as P


F32, BF16 = jnp.float32, jnp.bfloat16
HBM = pl.BlockSpec(memory_space=pltpu.HBM)
VMEM = pl.BlockSpec(memory_space=pltpu.VMEM)
CORES = 2
HOP_ONE, HOP_TWO, HOP_LAST = (1, 3, 0, 2), (2, 0, 3, 1), (3, 2, 1, 0)
SEND_ONE = ((1, 0), (3, 1), (0, 2), (2, 3))
SEND_TWO = ((2, 0), (0, 1), (3, 2), (1, 3))
SEND_ENDS, SEND_MIDDLE = ((1, 0), (2, 3)), ((1, 2), (2, 1))


def split(x):
    high = x.astype(BF16)
    return high, (x - high.astype(F32)).astype(BF16)


def dot(left, right):
    return jnp.dot(left, right, preferred_element_type=F32)


def dot3(left, right):
    (lh, ll), (rh, rl) = left, right
    return dot(lh, rh) + dot(lh, rl) + dot(ll, rh)


def eye(rows, cols, first):
    row = lax.broadcasted_iota(jnp.int32, (rows, cols), 0)
    col = lax.broadcasted_iota(jnp.int32, (rows, cols), 1)
    return jnp.where(row == col + first, 1.0, 0.0).astype(F32)


def each(n, body):
    step = min(256, n)
    for first in range(0, n, step):
        body(pl.ds(first, step), first)


def put(pair, cols, x):
    pair[0][:, cols], pair[1][:, cols] = split(x)


def product(left, right, cols):
    return dot3((left[0][...], left[1][...]), (right[0][:, cols], right[1][:, cols]))


def powers(n, x, e, f, g):
    def square(cols, _):
        s = product(e, e, cols)
        put(f, cols, s)
        x[:, cols] = x[:, cols] + s

    each(n, square)
    each(n, lambda cols, _: put(g, cols, x[:, cols] + product(e, f, cols)))


def first_kernel(pivot, g1h, g1l, vh, vl, lowh, lowl, rest, a, u, l, eh, el, fh, fl, uh, ul, sems):
    n = a.shape[0]
    g1, v, low, e, f, up = (g1h, g1l), (vh, vl), (lowh, lowl), (eh, el), (fh, fl), (uh, ul)
    copies = [
        pltpu.make_async_copy(pivot.at[pl.ds(i * n, n), pl.ds(j * n, n)], block, sems.at[2 * i + j])
        for i, j, block in ((0, 0, a), (0, 1, u), (1, 0, l), (1, 1, rest))
    ]
    for copy in copies:
        copy.start()

    def residual(cols, first):
        x = eye(n, cols.size, first) - a[:, cols]
        a[:, cols] = x
        put(e, cols, x)

    copies[0].wait()
    each(n, residual)
    powers(n, a, e, f, g1)
    copies[1].wait()
    each(n, lambda cols, _: put(up, cols, u[:, cols]))
    each(n, lambda cols, _: put(v, cols, u[:, cols] + product(g1, up, cols)))
    copies[2].wait()
    each(n, lambda cols, _: put(low, cols, l[:, cols]))
    copies[3].wait()

    def complement(cols, first):
        rest[:, cols] = eye(n, cols.size, first) - rest[:, cols]

    each(n, complement)


def first_part(pivot):
    n = pivot.shape[0] // 2
    half = jax.ShapeDtypeStruct((n, n), BF16)
    return pl.pallas_call(
        first_kernel,
        out_shape=(half,) * 6 + (jax.ShapeDtypeStruct((n, n), F32),),
        in_specs=[HBM],
        out_specs=(VMEM,) * 7,
        scratch_shapes=[pltpu.VMEM((n, n), F32)] * 3 + [pltpu.VMEM((n, n), BF16)] * 6 + [pltpu.SemaphoreType.DMA((4,))],
        cost_estimate=pl.CostEstimate(flops=18 * n * n * n, bytes_accessed=32 * n * n, transcendentals=0),
        compiler_params=pltpu.CompilerParams(vmem_limit_bytes=24 << 20),
        name="first_part",
    )(pivot)


def second_kernel(vh, vl, lowh, lowl, rest, g2h, g2l, d, eh, el, fh, fl):
    n = d.shape[0]
    v, low, g2, e, f = (vh, vl), (lowh, lowl), (g2h, g2l), (eh, el), (fh, fl)

    def residual(cols, _):
        x = rest[:, cols] + product(low, v, cols)
        d[:, cols] = x
        put(e, cols, x)

    each(n, residual)
    powers(n, d, e, f, g2)


def second_part(v, low, rest):
    n = rest.shape[0]
    half = jax.ShapeDtypeStruct((n, n), BF16)
    return pl.pallas_call(
        second_kernel,
        out_shape=(half,) * 2,
        in_specs=[VMEM] * 5,
        out_specs=(VMEM,) * 2,
        scratch_shapes=[pltpu.VMEM((n, n), F32)] + [pltpu.VMEM((n, n), BF16)] * 4,
        cost_estimate=pl.CostEstimate(flops=18 * n * n * n, bytes_accessed=16 * n * n, transcendentals=0),
        compiler_params=pltpu.CompilerParams(vmem_limit_bytes=24 << 20),
        name="second_part",
    )(*v, *low, rest)


def chain_kernel(g1h, g1l, vh, vl, lowh, lowl, g2h, g2l, *refs):
    rows, (yh, yl, r, rh, rl) = refs[:-5], refs[-5:]
    n = g1h.shape[0]
    deep = rows[0].shape[0]
    me = lax.axis_index("row")
    for s, piece in enumerate(rows):
        at = pl.ds(pl.multiple_of((me ^ s) * deep, deep), deep)
        x = piece[...]
        r[at, :] = x
        rh[at, :], rl[at, :] = split(x)
    upper, lower = pl.ds(0, n), pl.ds(n, n)
    full = lambda high, low: (high[...], low[...])
    ya = r[upper, :] + dot3(full(g1h, g1l), (rh[upper, :], rl[upper, :]))
    t2 = r[lower, :] - dot3(full(lowh, lowl), split(ya))
    y2 = split(t2 + dot3(full(g2h, g2l), split(t2)))
    yh[lower, :], yl[lower, :] = y2
    yh[upper, :], yl[upper, :] = split(ya - dot3(full(vh, vl), y2))


def chain_part(g1, v, low, g2, rows):
    n = g1[0].shape[0]
    width = rows[0].shape[1]
    half = jax.ShapeDtypeStruct((2 * n, width), BF16)
    return pl.pallas_call(
        chain_kernel,
        out_shape=(half,) * 2,
        in_specs=[VMEM] * (8 + len(rows)),
        out_specs=(VMEM,) * 2,
        scratch_shapes=[pltpu.VMEM((2 * n, width), F32)] + [pltpu.VMEM((2 * n, width), BF16)] * 2,
        cost_estimate=pl.CostEstimate(flops=24 * n * n * width, bytes_accessed=16 * n * (n + width), transcendentals=0),
        compiler_params=pltpu.CompilerParams(vmem_limit_bytes=16 << 20),
        name="chain_part",
    )(*g1, *v, *low, *g2, *rows)


def position():
    me = lax.axis_index("col")
    return me // CORES, me % CORES


def entry(table, index):
    value = jnp.int32(table[0])
    for i, x in enumerate(table[1:], 1):
        value = jnp.where(index == i, x, value)
    return value


def times(table, own, other, yh, yl):
    chip, core = position()
    tall = CORES * own.shape[1]
    at = pl.ds(pl.multiple_of(entry(table, chip) * tall, tall), tall)
    both = jnp.concatenate([jnp.where(core == 0, own, other), jnp.where(core == 0, other, own)], axis=1)
    return dot3(split(both), (yh[at, :], yl[at, :]))


def update_kernel(tables, trail, yh, yl, *refs):
    pieces, out = refs[:-1], refs[-1]
    total = trail[...]
    for i, table in enumerate(tables):
        total = total - times(table, pieces[2 * i][...], pieces[2 * i + 1][...], yh, yl)
    out[...] = total


def update_part(tables, trail, y, pieces):
    m, width = trail.shape
    wide = pieces[0].shape[1]
    return pl.pallas_call(
        functools.partial(update_kernel, tables),
        out_shape=jax.ShapeDtypeStruct((m, width), F32),
        in_specs=[VMEM] * (3 + len(pieces)),
        out_specs=VMEM,
        cost_estimate=pl.CostEstimate(
            flops=6 * m * width * wide * len(pieces), bytes_accessed=4 * m * (2 * width + wide * len(pieces)), transcendentals=0
        ),
        compiler_params=pltpu.CompilerParams(vmem_limit_bytes=16 << 20),
        name="update_part",
    )(trail, *y, *pieces)


def last_kernel(part, yh, yl, end, middle, end_other, middle_other, out):
    chip, _ = position()
    inner = (chip != 0) & (chip != len(HOP_LAST) - 1)
    own = jnp.where(inner, middle[...], end[...])
    other = jnp.where(inner, middle_other[...], end_other[...])
    out[...] = part[...] - times(HOP_LAST, own, other, yh, yl)


def last_part(part, y, *pieces):
    m, width = part.shape
    wide = pieces[0].shape[1]
    return pl.pallas_call(
        last_kernel,
        out_shape=jax.ShapeDtypeStruct((m, width), F32),
        in_specs=[VMEM] * 7,
        out_specs=VMEM,
        cost_estimate=pl.CostEstimate(flops=12 * m * width * wide, bytes_accessed=4 * m * (2 * width + 4 * wide), transcendentals=0),
        compiler_params=pltpu.CompilerParams(vmem_limit_bytes=8 << 20),
        name="last_part",
    )(part, *y, *pieces)


def local(n_row, pivot, col_panel, row_panel, trailing):
    def send(x, pairs):
        return lax.ppermute(x, "col", [(CORES * a + c, CORES * b + c) for a, b in pairs for c in range(CORES)])

    def exchange(x, chips):
        return lax.ppermute(x, "col", [(CORES * a + c, CORES * a + (c ^ 1)) for a in chips for c in range(CORES)])

    def row(s):
        return lax.ppermute(row_panel, "row", [(i, i ^ s) for i in range(n_row)])

    chips = tuple(range(len(HOP_ONE)))
    ends, inner = (chips[0], chips[-1]), chips[1:-1]
    one = send(col_panel, SEND_ONE)
    two = send(col_panel, SEND_TWO)
    end = send(one, SEND_ENDS)
    middle = send(col_panel, SEND_MIDDLE)
    rows = [row_panel] + [row(s) for s in range(1, n_row)]
    *pairs, rest = first_part(pivot)
    g1, v, low = pairs[0:2], pairs[2:4], pairs[4:6]
    g2 = second_part(v, low, rest)
    y = chain_part(g1, v, low, g2, rows)
    pieces = [x for mine in (col_panel, one, two) for x in (mine, exchange(mine, chips))]
    part = update_part((chips, HOP_ONE, HOP_TWO), trailing, y, pieces)
    end_other, middle_other = exchange(end, ends), exchange(middle, inner)
    return last_part(part, y, end, middle, end_other, middle_other)


def exact(left, right):
    return jnp.dot(left, right, precision=lax.Precision.HIGHEST, preferred_element_type=F32)


def newton_inverse(matrix):
    identity = jnp.eye(matrix.shape[0], dtype=F32)
    initial = 2.0 * identity - matrix
    return exact(initial, 2.0 * identity - exact(matrix, initial))


def gathered(pivot, col_panel, row_panel, trailing):
    cols = lax.all_gather(col_panel, "col", axis=1, tiled=True)
    rows = lax.all_gather(row_panel, "row", axis=0, tiled=True)
    n = pivot.shape[0] // 2
    top_left, top_right, low_left, low_right = pivot[:n, :n], pivot[:n, n:], pivot[n:, :n], pivot[n:, n:]
    inverse_one = newton_inverse(top_left)
    multiplier = exact(low_left, inverse_one)
    inverse_two = newton_inverse(low_right - exact(multiplier, top_right))
    factor_one = exact(cols[:, :n], inverse_one)
    factor_two = exact(cols[:, n:] - exact(factor_one, top_right), inverse_two)
    rows_two = rows[n:] - exact(multiplier, rows[:n])
    return trailing - exact(factor_one, rows[:n]) - exact(factor_two, rows_two)


def power_of_two(n):
    return n & (n - 1) == 0


def solution(mesh):
    n_row, n_col = mesh.shape["row"], mesh.shape["col"]
    line = n_col == CORES * len(HOP_ONE) and power_of_two(n_row)

    def body(pivot, col_panel, row_panel, trailing):
        if line:
            return local(n_row, pivot, col_panel, row_panel, trailing)
        return gathered(pivot, col_panel, row_panel, trailing)

    return jax.shard_map(
        body,
        mesh=mesh,
        in_specs=(P(), P("row", "col"), P("row", "col"), P("row", "col")),
        out_specs=P("row", "col"),
        check_vma=False,
    )
```

```python
import functools

import jax
import jax.numpy as jnp
from jax import lax
from jax.experimental import pallas as pl
from jax.experimental.pallas import tpu as pltpu
from jax.sharding import PartitionSpec as P


F32, BF16 = jnp.float32, jnp.bfloat16
VMEM = pl.BlockSpec(memory_space=pltpu.VMEM)
CORES = 2
HOP_ONE, HOP_TWO, HOP_LAST = (1, 3, 0, 2), (2, 0, 3, 1), (3, 2, 1, 0)
SEND_ONE = ((1, 0), (3, 1), (0, 2), (2, 3))
SEND_TWO = ((2, 0), (0, 1), (3, 2), (1, 3))
SEND_ENDS = ((1, 0), (2, 3), (0, 1), (3, 2))
SEND_MIDDLE = ((1, 2), (2, 1), (0, 0), (3, 3))


def split(x):
    high = x.astype(BF16)
    return high, (x - high.astype(F32)).astype(BF16)


def dot(left, right):
    return jnp.dot(left, right, preferred_element_type=F32)


def dot3(left, right):
    (lh, ll), (rh, rl) = left, right
    return dot(lh, rh) + dot(lh, rl) + dot(ll, rh)


def eye(rows, cols, first):
    row = lax.broadcasted_iota(jnp.int32, (rows, cols), 0)
    col = lax.broadcasted_iota(jnp.int32, (rows, cols), 1)
    return jnp.where(row == col + first, 1.0, 0.0).astype(F32)


def each(n, body):
    step = min(256, n)
    for first in range(0, n, step):
        body(pl.ds(first, step), first)


def put(pair, cols, x):
    pair[0][:, cols], pair[1][:, cols] = split(x)


def product(left, right, cols):
    return dot3((left[0][...], left[1][...]), (right[0][:, cols], right[1][:, cols]))


def powers(n, x, e, f, g):
    def square(cols, _):
        s = product(e, e, cols)
        put(f, cols, s)
        x[:, cols] = x[:, cols] + s

    each(n, square)
    each(n, lambda cols, _: put(g, cols, x[:, cols] + product(e, f, cols)))


def quadrant(n, i, j):
    return pl.ds(i * n, n), pl.ds(j * n, n)


def first_kernel(pivot, g1h, g1l, u, l, d, a, eh, el, fh, fl, sems):
    n = a.shape[0]
    copies = [
        pltpu.make_async_copy(pivot.at[quadrant(n, i, j)], block, sems.at[2 * i + j])
        for i, j, block in ((0, 0, a), (0, 1, u), (1, 0, l), (1, 1, d))
    ]
    for copy in copies:
        copy.start()
    copies[0].wait()

    def residual(cols, first):
        x = eye(n, cols.size, first) - a[:, cols]
        a[:, cols] = x
        put((eh, el), cols, x)

    each(n, residual)
    powers(n, a, (eh, el), (fh, fl), (g1h, g1l))
    for copy in copies[1:]:
        copy.wait()


def kernel_call(body, name, outs, ins, scratch, products, limit=16):
    n = outs[0].shape[0]
    specs = [pl.BlockSpec(memory_space=pltpu.HBM if name == "first_part" else pltpu.VMEM)] * len(ins)
    return pl.pallas_call(
        body,
        out_shape=tuple(outs),
        in_specs=specs,
        out_specs=(VMEM,) * len(outs),
        scratch_shapes=scratch,
        cost_estimate=pl.CostEstimate(flops=int(6 * products * n * n * n), bytes_accessed=16 * n * n, transcendentals=0),
        compiler_params=pltpu.CompilerParams(vmem_limit_bytes=limit << 20),
    )(*ins)


def half(*shape):
    return jax.ShapeDtypeStruct(shape, BF16)


def single(*shape):
    return jax.ShapeDtypeStruct(shape, F32)


def first_part(pivot):
    n = pivot.shape[0] // 2
    outs = [half(n, n)] * 2 + [single(n, n)] * 3
    scratch = [pltpu.VMEM((n, n), F32)] + [pltpu.VMEM((n, n), BF16)] * 4 + [pltpu.SemaphoreType.DMA((4,))]
    pivot = pltpu.with_memory_space_constraint(pivot, pltpu.HBM)
    return kernel_call(first_kernel, "first_part", outs, (pivot,), scratch, 2)


def second_kernel(g1h, g1l, u, l, d, vh, vl, lowh, lowl, e, eh, el, uh, ul):
    n = u.shape[0]
    g1, v, low, up = (g1h, g1l), (vh, vl), (lowh, lowl), (uh, ul)
    each(n, lambda cols, _: put(up, cols, u[:, cols]))
    each(n, lambda cols, _: put(v, cols, u[:, cols] + product(g1, up, cols)))
    each(n, lambda cols, _: put(low, cols, l[:, cols]))

    def residual(cols, first):
        x = (eye(n, cols.size, first) - d[:, cols]) + product(low, v, cols)
        e[:, cols] = x
        put((eh, el), cols, x)

    each(n, residual)


def second_part(g1, u, l, d):
    n = u.shape[0]
    outs = [half(n, n)] * 4 + [single(n, n)] + [half(n, n)] * 2
    return kernel_call(second_kernel, "second_part", outs, (*g1, u, l, d), [pltpu.VMEM((n, n), BF16)] * 2, 2)


def third_kernel(e, eh, el, g2h, g2l, x, fh, fl):
    n = e.shape[0]
    x[...] = e[...]
    powers(n, x, (eh, el), (fh, fl), (g2h, g2l))


def third_part(e, eh, el):
    n = e.shape[0]
    scratch = [pltpu.VMEM((n, n), F32)] + [pltpu.VMEM((n, n), BF16)] * 2
    return kernel_call(third_kernel, "third_part", [half(n, n)] * 2, (e, eh, el), scratch, 2)


def chain_kernel(g1h, g1l, vh, vl, lowh, lowl, g2h, g2l, *refs):
    rows, (yh, yl, r, rh, rl) = refs[:-5], refs[-5:]
    n = g1h.shape[0]
    deep = rows[0].shape[0]
    me = lax.axis_index("row")
    for s, piece in enumerate(rows):
        at = pl.ds(pl.multiple_of((me ^ s) * deep, deep), deep)
        x = piece[...]
        r[at, :] = x
        rh[at, :], rl[at, :] = split(x)
    upper, lower = pl.ds(0, n), pl.ds(n, n)
    full = lambda high, low: (high[...], low[...])
    ya = r[upper, :] + dot3(full(g1h, g1l), (rh[upper, :], rl[upper, :]))
    t2 = r[lower, :] - dot3(full(lowh, lowl), split(ya))
    y2 = split(t2 + dot3(full(g2h, g2l), split(t2)))
    yh[lower, :], yl[lower, :] = y2
    yh[upper, :], yl[upper, :] = split(ya - dot3(full(vh, vl), y2))


def chain_part(g1, v, low, g2, rows):
    n = g1[0].shape[0]
    width = rows[0].shape[1]
    return pl.pallas_call(
        chain_kernel,
        out_shape=(half(2 * n, width),) * 2,
        in_specs=[VMEM] * (8 + len(rows)),
        out_specs=(VMEM,) * 2,
        scratch_shapes=[pltpu.VMEM((2 * n, width), F32)] + [pltpu.VMEM((2 * n, width), BF16)] * 2,
        cost_estimate=pl.CostEstimate(flops=24 * n * n * width, bytes_accessed=16 * n * (n + width), transcendentals=0),
        compiler_params=pltpu.CompilerParams(vmem_limit_bytes=16 << 20),
        name="chain_part",
    )(*g1, *v, *low, *g2, *rows)


def position():
    me = lax.axis_index("col")
    return me // CORES, me % CORES


def entry(table, index):
    value = jnp.int32(table[0])
    for i, x in enumerate(table[1:], 1):
        value = jnp.where(index == i, x, value)
    return value


def times(table, own, other, yh, yl):
    chip, core = position()
    tall = CORES * own.shape[1]
    at = pl.ds(pl.multiple_of(entry(table, chip) * tall, tall), tall)
    both = jnp.concatenate([jnp.where(core == 0, own, other), jnp.where(core == 0, other, own)], axis=1)
    return dot3(split(both), (yh[at, :], yl[at, :]))


def update_kernel(tables, trail, yh, yl, *refs):
    pieces, out = refs[:-1], refs[-1]
    total = trail[...]
    for i, table in enumerate(tables):
        total = total - times(table, pieces[2 * i][...], pieces[2 * i + 1][...], yh, yl)
    out[...] = total


def update_part(tables, trail, y, pieces):
    m, width = trail.shape
    wide = pieces[0].shape[1]
    return pl.pallas_call(
        functools.partial(update_kernel, tables),
        out_shape=jax.ShapeDtypeStruct((m, width), F32),
        in_specs=[VMEM] * (3 + len(pieces)),
        out_specs=VMEM,
        cost_estimate=pl.CostEstimate(
            flops=6 * m * width * wide * len(pieces), bytes_accessed=4 * m * (2 * width + wide * len(pieces)), transcendentals=0
        ),
        compiler_params=pltpu.CompilerParams(vmem_limit_bytes=16 << 20),
        name="update_part",
    )(trail, *y, *pieces)


def last_kernel(part, yh, yl, end, middle, end_other, middle_other, out):
    chip, _ = position()
    inner = (chip != 0) & (chip != len(HOP_LAST) - 1)
    own = jnp.where(inner, middle[...], end[...])
    other = jnp.where(inner, middle_other[...], end_other[...])
    out[...] = part[...] - times(HOP_LAST, own, other, yh, yl)


def last_part(part, y, *pieces):
    m, width = part.shape
    wide = pieces[0].shape[1]
    return pl.pallas_call(
        last_kernel,
        out_shape=jax.ShapeDtypeStruct((m, width), F32),
        in_specs=[VMEM] * 7,
        out_specs=VMEM,
        cost_estimate=pl.CostEstimate(flops=12 * m * width * wide, bytes_accessed=4 * m * (2 * width + 4 * wide), transcendentals=0),
        compiler_params=pltpu.CompilerParams(vmem_limit_bytes=8 << 20),
        name="last_part",
    )(part, *y, *pieces)


def local(n_row, pivot, col_panel, row_panel, trailing):
    def send(x, pairs):
        return lax.ppermute(x, "col", [(CORES * a + c, CORES * b + c) for a, b in pairs for c in range(CORES)])

    def exchange(x, chips):
        return lax.ppermute(x, "col", [(CORES * a + c, CORES * a + (c ^ 1)) for a in chips for c in range(CORES)])

    def row(s):
        return lax.ppermute(row_panel, "row", [(i, i ^ s) for i in range(n_row)])

    chips = tuple(range(len(HOP_ONE)))
    one = send(col_panel, SEND_ONE)
    two = send(col_panel, SEND_TWO)
    end = send(one, SEND_ENDS)
    middle = send(col_panel, SEND_MIDDLE)
    rows = [row_panel] + [row(s) for s in range(1, n_row)]
    *g1, u, l, d = first_part(pivot)
    vh, vl, lowh, lowl, *e = second_part(g1, u, l, d)
    g2 = third_part(*e)
    y = chain_part(g1, (vh, vl), (lowh, lowl), g2, rows)
    pieces = [x for mine in (col_panel, one, two) for x in (mine, exchange(mine, chips))]
    part = update_part((chips, HOP_ONE, HOP_TWO), trailing, y, pieces)
    end_other, middle_other = exchange(end, chips), exchange(middle, chips)
    return last_part(part, y, end, middle, end_other, middle_other)


def exact(left, right):
    return jnp.dot(left, right, precision=lax.Precision.HIGHEST, preferred_element_type=F32)


def newton_inverse(matrix):
    identity = jnp.eye(matrix.shape[0], dtype=F32)
    initial = 2.0 * identity - matrix
    return exact(initial, 2.0 * identity - exact(matrix, initial))


def gathered(pivot, col_panel, row_panel, trailing):
    cols = lax.all_gather(col_panel, "col", axis=1, tiled=True)
    rows = lax.all_gather(row_panel, "row", axis=0, tiled=True)
    n = pivot.shape[0] // 2
    top_left, top_right, low_left, low_right = pivot[:n, :n], pivot[:n, n:], pivot[n:, :n], pivot[n:, n:]
    inverse_one = newton_inverse(top_left)
    multiplier = exact(low_left, inverse_one)
    inverse_two = newton_inverse(low_right - exact(multiplier, top_right))
    factor_one = exact(cols[:, :n], inverse_one)
    factor_two = exact(cols[:, n:] - exact(factor_one, top_right), inverse_two)
    rows_two = rows[n:] - exact(multiplier, rows[:n])
    return trailing - exact(factor_one, rows[:n]) - exact(factor_two, rows_two)


def power_of_two(n):
    return n & (n - 1) == 0


def solution(mesh):
    n_row, n_col = mesh.shape["row"], mesh.shape["col"]
    line = n_col == CORES * len(HOP_ONE) and power_of_two(n_row)

    def body(pivot, col_panel, row_panel, trailing):
        if line:
            return local(n_row, pivot, col_panel, row_panel, trailing)
        return gathered(pivot, col_panel, row_panel, trailing)

    return jax.shard_map(
        body,
        mesh=mesh,
        in_specs=(P(), P("row", "col"), P("row", "col"), P("row", "col")),
        out_specs=P("row", "col"),
        check_vma=False,
    )
```

```python
import functools

import jax
import jax.numpy as jnp
from jax import lax
from jax.experimental import pallas as pl
from jax.experimental.pallas import tpu as pltpu
from jax.sharding import PartitionSpec as P


F32, BF16 = jnp.float32, jnp.bfloat16
VMEM = pl.BlockSpec(memory_space=pltpu.VMEM)
CHUNK, LAST_CHUNK = 256, 128
CORES = 2
HOP_ONE, HOP_TWO, HOP_LAST = (1, 3, 0, 2), (2, 0, 3, 1), (3, 2, 1, 0)
SEND_ONE = ((1, 0), (3, 1), (0, 2), (2, 3))
SEND_TWO = ((2, 0), (0, 1), (3, 2), (1, 3))
SEND_ENDS = ((1, 0), (2, 3), (0, 1), (3, 2))
SEND_MIDDLE = ((1, 2), (2, 1))


def split(x):
    high = x.astype(BF16)
    return high, (x - high.astype(F32)).astype(BF16)


def dot(left, right):
    return jnp.dot(left, right, preferred_element_type=F32)


def dot3(left, right):
    (lh, ll), (rh, rl) = left, right
    return dot(lh, rh) + dot(lh, rl) + dot(ll, rh)


def eye(rows, cols, first):
    row = lax.broadcasted_iota(jnp.int32, (rows, cols), 0)
    col = lax.broadcasted_iota(jnp.int32, (rows, cols), 1)
    return jnp.where(row == col + first, 1.0, 0.0).astype(F32)


def each(n, body):
    step = min(256, n)
    for first in range(0, n, step):
        body(pl.ds(first, step), first)


def put(pair, cols, x):
    pair[0][:, cols], pair[1][:, cols] = split(x)


def product(left, right, cols):
    return dot3((left[0][...], left[1][...]), (right[0][:, cols], right[1][:, cols]))


def powers(n, x, e, f, g):
    def square(cols, _):
        s = product(e, e, cols)
        put(f, cols, s)
        x[:, cols] = x[:, cols] + s

    each(n, square)
    each(n, lambda cols, _: put(g, cols, x[:, cols] + product(e, f, cols)))


def quadrant(n, i, j):
    return pl.ds(i * n, n), pl.ds(j * n, n)


def first_kernel(pivot, g1h, g1l, u, l, d, a, eh, el, fh, fl, sems):
    n = a.shape[0]
    copies = [
        pltpu.make_async_copy(pivot.at[quadrant(n, i, j)], block, sems.at[2 * i + j])
        for i, j, block in ((0, 0, a), (0, 1, u), (1, 0, l), (1, 1, d))
    ]
    for copy in copies:
        copy.start()
    copies[0].wait()

    def residual(cols, first):
        x = eye(n, cols.size, first) - a[:, cols]
        a[:, cols] = x
        put((eh, el), cols, x)

    each(n, residual)
    powers(n, a, (eh, el), (fh, fl), (g1h, g1l))
    for copy in copies[1:]:
        copy.wait()


def kernel_call(body, name, outs, ins, scratch, products, limit=16):
    n = outs[0].shape[0]
    specs = [pl.BlockSpec(memory_space=pltpu.HBM if name == "first_part" else pltpu.VMEM)] * len(ins)
    return pl.pallas_call(
        body,
        out_shape=tuple(outs),
        in_specs=specs,
        out_specs=(VMEM,) * len(outs),
        scratch_shapes=scratch,
        cost_estimate=pl.CostEstimate(flops=int(6 * products * n * n * n), bytes_accessed=16 * n * n, transcendentals=0),
        compiler_params=pltpu.CompilerParams(vmem_limit_bytes=limit << 20),
    )(*ins)


def half(*shape):
    return jax.ShapeDtypeStruct(shape, BF16)


def single(*shape):
    return jax.ShapeDtypeStruct(shape, F32)


def first_part(pivot):
    n = pivot.shape[0] // 2
    outs = [half(n, n)] * 2 + [single(n, n)] * 3
    scratch = [pltpu.VMEM((n, n), F32)] + [pltpu.VMEM((n, n), BF16)] * 4 + [pltpu.SemaphoreType.DMA((4,))]
    pivot = pltpu.with_memory_space_constraint(pivot, pltpu.HBM)
    return kernel_call(first_kernel, "first_part", outs, (pivot,), scratch, 2)


def second_kernel(g1h, g1l, u, l, d, vh, vl, lowh, lowl, e, eh, el, uh, ul):
    n = u.shape[0]
    g1, v, low, up = (g1h, g1l), (vh, vl), (lowh, lowl), (uh, ul)
    each(n, lambda cols, _: put(up, cols, u[:, cols]))
    each(n, lambda cols, _: put(v, cols, u[:, cols] + product(g1, up, cols)))
    each(n, lambda cols, _: put(low, cols, l[:, cols]))

    def residual(cols, first):
        x = (eye(n, cols.size, first) - d[:, cols]) + product(low, v, cols)
        e[:, cols] = x
        put((eh, el), cols, x)

    each(n, residual)


def second_part(g1, u, l, d):
    n = u.shape[0]
    outs = [half(n, n)] * 4 + [single(n, n)] + [half(n, n)] * 2
    return kernel_call(second_kernel, "second_part", outs, (*g1, u, l, d), [pltpu.VMEM((n, n), BF16)] * 2, 2)


def third_kernel(e, eh, el, g2h, g2l, x, fh, fl):
    n = e.shape[0]
    x[...] = e[...]
    powers(n, x, (eh, el), (fh, fl), (g2h, g2l))


def third_part(e, eh, el):
    n = e.shape[0]
    scratch = [pltpu.VMEM((n, n), F32)] + [pltpu.VMEM((n, n), BF16)] * 2
    return kernel_call(third_kernel, "third_part", [half(n, n)] * 2, (e, eh, el), scratch, 2)


def chain_kernel(g1h, g1l, vh, vl, lowh, lowl, g2h, g2l, *refs):
    rows, (yh, yl, r, rh, rl, f, fh, fl) = refs[:-8], refs[-8:]
    n = g1h.shape[0]
    deep = rows[0].shape[0]
    step = min(CHUNK, n)
    me = lax.axis_index("row")
    for s, piece in enumerate(rows):
        at = pl.ds(pl.multiple_of((me ^ s) * deep, deep), deep)
        x = piece[...]
        r[at, :] = x
        rh[at, :], rl[at, :] = split(x)

    def phase(left, right, finish):
        for first in range(0, n, step):
            at = pl.ds(first, step)
            finish(first, at, dot3((left[0][at, :], left[1][at, :]), right))

    def inner(first, at, p):
        x = r[at, :] + p
        f[at, :] = x
        fh[at, :], fl[at, :] = split(x)

    def residual(first, at, p):
        x = r[pl.ds(n + first, step), :] - p
        r[pl.ds(n + first, step), :] = x
        rh[at, :], rl[at, :] = split(x)

    def lower(first, at, p):
        to = pl.ds(n + first, step)
        yh[to, :], yl[to, :] = split(r[to, :] + p)

    def upper(first, at, p):
        yh[at, :], yl[at, :] = split(f[at, :] - p)

    phase((g1h, g1l), (rh[pl.ds(0, n), :], rl[pl.ds(0, n), :]), inner)
    phase((lowh, lowl), (fh[...], fl[...]), residual)
    phase((g2h, g2l), (rh[pl.ds(0, n), :], rl[pl.ds(0, n), :]), lower)
    phase((vh, vl), (yh[pl.ds(n, n), :], yl[pl.ds(n, n), :]), upper)


def chain_part(g1, v, low, g2, rows):
    n = g1[0].shape[0]
    width = rows[0].shape[1]
    return pl.pallas_call(
        chain_kernel,
        out_shape=(half(2 * n, width),) * 2,
        in_specs=[VMEM] * (8 + len(rows)),
        out_specs=(VMEM,) * 2,
        scratch_shapes=[pltpu.VMEM((2 * n, width), F32)]
        + [pltpu.VMEM((2 * n, width), BF16)] * 2
        + [pltpu.VMEM((n, width), F32)]
        + [pltpu.VMEM((n, width), BF16)] * 2,
        cost_estimate=pl.CostEstimate(flops=24 * n * n * width, bytes_accessed=16 * n * (n + width), transcendentals=0),
        compiler_params=pltpu.CompilerParams(vmem_limit_bytes=16 << 20),
        name="chain_part",
    )(*g1, *v, *low, *g2, *rows)


def position():
    me = lax.axis_index("col")
    return me // CORES, me % CORES


def entry(table, index):
    value = jnp.int32(table[0])
    for i, x in enumerate(table[1:], 1):
        value = jnp.where(index == i, x, value)
    return value


def times(table, own, other, yh, yl):
    chip, core = position()
    tall = CORES * own.shape[1]
    at = pl.ds(pl.multiple_of(entry(table, chip) * tall, tall), tall)
    both = jnp.concatenate([jnp.where(core == 0, own, other), jnp.where(core == 0, other, own)], axis=1)
    return dot3(split(both), (yh[at, :], yl[at, :]))


def chosen(middle, end):
    chip, _ = position()
    return jnp.where((chip != 0) & (chip != len(HOP_LAST) - 1), middle, end)


def narrow(shard, other, yh, yl):
    chip, core = position()
    wide = shard.shape[1]
    at = pl.ds(pl.multiple_of(entry(HOP_LAST, chip) * CORES * wide + (core ^ other) * wide, wide), wide)
    return dot3(split(shard), (yh[at, :], yl[at, :]))


def update_kernel(tables, trail, yh, yl, *refs):
    (*pieces, middle, end), out = refs[:-1], refs[-1]
    total = trail[...]
    for i, table in enumerate(tables):
        total = total - times(table, pieces[2 * i][...], pieces[2 * i + 1][...], yh, yl)
    out[...] = total - narrow(chosen(middle[...], end[...]), 0, yh, yl)


def update_part(tables, trail, y, pieces):
    m, width = trail.shape
    wide = pieces[0].shape[1]
    return pl.pallas_call(
        functools.partial(update_kernel, tables),
        out_shape=jax.ShapeDtypeStruct((m, width), F32),
        in_specs=[VMEM] * (3 + len(pieces)),
        out_specs=VMEM,
        cost_estimate=pl.CostEstimate(
            flops=6 * m * width * wide * len(pieces), bytes_accessed=4 * m * (2 * width + wide * len(pieces)), transcendentals=0
        ),
        compiler_params=pltpu.CompilerParams(vmem_limit_bytes=16 << 20),
        name="update_part",
    )(trail, *y, *pieces)


def last_kernel(part, yh, yl, middle, end, out, total, sems):
    m = part.shape[0]
    step = min(LAST_CHUNK, m)
    copies = []
    for i, first in enumerate(range(0, m, step)):
        at = pl.ds(first, step)
        total[at, :] = part[at, :] - narrow(chosen(middle[at, :], end[at, :]), 1, yh, yl)
        copies.append(pltpu.make_async_copy(total.at[at, :], out.at[at, :], sems.at[i]))
        copies[-1].start()
    for copy in copies:
        copy.wait()


def last_part(part, y, *pieces):
    m, width = part.shape
    wide = pieces[0].shape[1]
    return pl.pallas_call(
        last_kernel,
        out_shape=jax.ShapeDtypeStruct((m, width), F32),
        in_specs=[VMEM] * 5,
        out_specs=pl.BlockSpec(memory_space=pltpu.HBM),
        scratch_shapes=[pltpu.VMEM((m, width), F32), pltpu.SemaphoreType.DMA((-(-m // LAST_CHUNK),))],
        cost_estimate=pl.CostEstimate(flops=6 * m * width * wide, bytes_accessed=4 * m * (2 * width + 2 * wide), transcendentals=0),
        compiler_params=pltpu.CompilerParams(vmem_limit_bytes=8 << 20),
        name="last_part",
    )(part, *y, *pieces)


def local(n_row, pivot, col_panel, row_panel, trailing):
    chips = tuple(range(len(HOP_ONE)))

    def send(x, pairs):
        idle = set(chips) - {a for a, _ in pairs}
        hops = [(CORES * a + c, CORES * b + c) for a, b in pairs for c in range(CORES)]
        swaps = [(CORES * a + c, CORES * a + (c ^ 1)) for a in sorted(idle) for c in range(CORES)]
        return lax.ppermute(x, "col", hops + swaps)

    def exchange(x):
        return send(x, ())

    def row(s):
        return lax.ppermute(row_panel, "row", [(i, i ^ s) for i in range(n_row)])

    one = send(col_panel, SEND_ONE)
    two = send(col_panel, SEND_TWO)
    end = send(one, SEND_ENDS)
    middle = send(col_panel, SEND_MIDDLE)
    rows = [row_panel] + [row(s) for s in range(1, n_row)]
    *g1, u, l, d = first_part(pivot)
    vh, vl, lowh, lowl, *e = second_part(g1, u, l, d)
    g2 = third_part(*e)
    y = chain_part(g1, (vh, vl), (lowh, lowl), g2, rows)
    pieces = [x for mine in (col_panel, one, two) for x in (mine, exchange(mine))]
    part = update_part((chips, HOP_ONE, HOP_TWO), trailing, y, pieces + [middle, end])
    others = exchange(middle), exchange(end)
    return last_part(part, y, *others)


def exact(left, right):
    return jnp.dot(left, right, precision=lax.Precision.HIGHEST, preferred_element_type=F32)


def newton_inverse(matrix):
    identity = jnp.eye(matrix.shape[0], dtype=F32)
    initial = 2.0 * identity - matrix
    return exact(initial, 2.0 * identity - exact(matrix, initial))


def gathered(pivot, col_panel, row_panel, trailing):
    cols = lax.all_gather(col_panel, "col", axis=1, tiled=True)
    rows = lax.all_gather(row_panel, "row", axis=0, tiled=True)
    n = pivot.shape[0] // 2
    top_left, top_right, low_left, low_right = pivot[:n, :n], pivot[:n, n:], pivot[n:, :n], pivot[n:, n:]
    inverse_one = newton_inverse(top_left)
    multiplier = exact(low_left, inverse_one)
    inverse_two = newton_inverse(low_right - exact(multiplier, top_right))
    factor_one = exact(cols[:, :n], inverse_one)
    factor_two = exact(cols[:, n:] - exact(factor_one, top_right), inverse_two)
    rows_two = rows[n:] - exact(multiplier, rows[:n])
    return trailing - exact(factor_one, rows[:n]) - exact(factor_two, rows_two)


def power_of_two(n):
    return n & (n - 1) == 0


def solution(mesh):
    n_row, n_col = mesh.shape["row"], mesh.shape["col"]
    line = n_col == CORES * len(HOP_ONE) and power_of_two(n_row)

    def body(pivot, col_panel, row_panel, trailing):
        if line:
            return local(n_row, pivot, col_panel, row_panel, trailing)
        return gathered(pivot, col_panel, row_panel, trailing)

    return jax.shard_map(
        body,
        mesh=mesh,
        in_specs=(P(), P("row", "col"), P("row", "col"), P("row", "col")),
        out_specs=P("row", "col"),
        check_vma=False,
    )
```

```python
import functools

import jax
import jax.numpy as jnp
from jax import lax
from jax.experimental import pallas as pl
from jax.experimental.pallas import tpu as pltpu
from jax.sharding import PartitionSpec as P


F32, BF16 = jnp.float32, jnp.bfloat16
VMEM = pl.BlockSpec(memory_space=pltpu.VMEM)
CHUNK, TAIL = 256, 64
CORES = 2
HOP_ONE, HOP_TWO, HOP_LAST = (1, 3, 0, 2), (2, 0, 3, 1), (3, 2, 1, 0)
SEND_ONE = ((1, 0), (3, 1), (0, 2), (2, 3))
SEND_TWO = ((2, 0), (0, 1), (3, 2), (1, 3))
SEND_ENDS = ((1, 0), (2, 3), (0, 1), (3, 2))
SEND_MIDDLE = ((1, 2), (2, 1))


def split(x):
    high = x.astype(BF16)
    return high, (x - high.astype(F32)).astype(BF16)


def dot(left, right):
    return jnp.dot(left, right, preferred_element_type=F32)


def dot3(left, right):
    (lh, ll), (rh, rl) = left, right
    return dot(lh, rh) + dot(lh, rl) + dot(ll, rh)


def eye(rows, cols, first):
    row = lax.broadcasted_iota(jnp.int32, (rows, cols), 0)
    col = lax.broadcasted_iota(jnp.int32, (rows, cols), 1)
    return jnp.where(row == col + first, 1.0, 0.0).astype(F32)


def each(n, body):
    step = min(256, n)
    for first in range(0, n, step):
        body(pl.ds(first, step), first)


def put(pair, cols, x):
    pair[0][:, cols], pair[1][:, cols] = split(x)


def product(left, right, cols):
    return dot3((left[0][...], left[1][...]), (right[0][:, cols], right[1][:, cols]))


def powers(n, x, e, f, g):
    def square(cols, _):
        s = product(e, e, cols)
        put(f, cols, s)
        x[:, cols] = x[:, cols] + s

    each(n, square)
    each(n, lambda cols, _: put(g, cols, x[:, cols] + product(e, f, cols)))


def quadrant(n, i, j):
    return pl.ds(i * n, n), pl.ds(j * n, n)


def first_kernel(pivot, g1h, g1l, u, l, d, a, eh, el, fh, fl, sems):
    n = a.shape[0]
    copies = [
        pltpu.make_async_copy(pivot.at[quadrant(n, i, j)], block, sems.at[2 * i + j])
        for i, j, block in ((0, 0, a), (0, 1, u), (1, 0, l), (1, 1, d))
    ]
    for copy in copies:
        copy.start()
    copies[0].wait()

    def residual(cols, first):
        x = eye(n, cols.size, first) - a[:, cols]
        a[:, cols] = x
        put((eh, el), cols, x)

    each(n, residual)
    powers(n, a, (eh, el), (fh, fl), (g1h, g1l))
    for copy in copies[1:]:
        copy.wait()


def kernel_call(body, name, outs, ins, scratch, products, limit=16):
    n = outs[0].shape[0]
    specs = [pl.BlockSpec(memory_space=pltpu.HBM if name == "first_part" else pltpu.VMEM)] * len(ins)
    return pl.pallas_call(
        body,
        out_shape=tuple(outs),
        in_specs=specs,
        out_specs=(VMEM,) * len(outs),
        scratch_shapes=scratch,
        cost_estimate=pl.CostEstimate(flops=int(6 * products * n * n * n), bytes_accessed=16 * n * n, transcendentals=0),
        compiler_params=pltpu.CompilerParams(vmem_limit_bytes=limit << 20),
    )(*ins)


def half(*shape):
    return jax.ShapeDtypeStruct(shape, BF16)


def single(*shape):
    return jax.ShapeDtypeStruct(shape, F32)


def first_part(pivot):
    n = pivot.shape[0] // 2
    outs = [half(n, n)] * 2 + [single(n, n)] * 3
    scratch = [pltpu.VMEM((n, n), F32)] + [pltpu.VMEM((n, n), BF16)] * 4 + [pltpu.SemaphoreType.DMA((4,))]
    pivot = pltpu.with_memory_space_constraint(pivot, pltpu.HBM)
    return kernel_call(first_kernel, "first_part", outs, (pivot,), scratch, 2)


def second_kernel(g1h, g1l, u, l, d, shard, vh, vl, lowh, lowl, e, eh, el, head, uh, ul):
    n = u.shape[0]
    head[...] = shard[pl.ds(0, head.shape[0]), :]
    g1, v, low, up = (g1h, g1l), (vh, vl), (lowh, lowl), (uh, ul)
    each(n, lambda cols, _: put(up, cols, u[:, cols]))
    each(n, lambda cols, _: put(v, cols, u[:, cols] + product(g1, up, cols)))
    each(n, lambda cols, _: put(low, cols, l[:, cols]))

    def residual(cols, first):
        x = (eye(n, cols.size, first) - d[:, cols]) + product(low, v, cols)
        e[:, cols] = x
        put((eh, el), cols, x)

    each(n, residual)


def second_part(g1, u, l, d, shard):
    n = u.shape[0]
    m, wide = shard.shape
    outs = [half(n, n)] * 4 + [single(n, n)] + [half(n, n)] * 2 + [single(m - TAIL, wide)]
    return kernel_call(second_kernel, "second_part", outs, (*g1, u, l, d, shard), [pltpu.VMEM((n, n), BF16)] * 2, 2)


def third_kernel(e, eh, el, own, other, g2h, g2l, tails, x, fh, fl):
    n = e.shape[0]
    for i, shard in enumerate((own, other)):
        tails[pl.ds(i * TAIL, TAIL), :] = shard[pl.ds(shard.shape[0] - TAIL, TAIL), :]
    x[...] = e[...]
    powers(n, x, (eh, el), (fh, fl), (g2h, g2l))


def third_part(e, own, other):
    n = e[0].shape[0]
    outs = [half(n, n)] * 2 + [single(2 * TAIL, own.shape[1])]
    scratch = [pltpu.VMEM((n, n), F32)] + [pltpu.VMEM((n, n), BF16)] * 2
    return kernel_call(third_kernel, "third_part", outs, (*e, own, other), scratch, 2)


def chain_kernel(g1h, g1l, vh, vl, lowh, lowl, g2h, g2l, *refs):
    rows, (yh, yl, r, rh, rl, f, fh, fl) = refs[:-8], refs[-8:]
    n = g1h.shape[0]
    deep = rows[0].shape[0]
    step = min(CHUNK, n)
    me = lax.axis_index("row")
    for s, piece in enumerate(rows):
        at = pl.ds(pl.multiple_of((me ^ s) * deep, deep), deep)
        x = piece[...]
        r[at, :] = x
        rh[at, :], rl[at, :] = split(x)

    def phase(left, right, finish):
        for first in range(0, n, step):
            at = pl.ds(first, step)
            finish(first, at, dot3((left[0][at, :], left[1][at, :]), right))

    def inner(first, at, p):
        x = r[at, :] + p
        f[at, :] = x
        fh[at, :], fl[at, :] = split(x)

    def residual(first, at, p):
        x = r[pl.ds(n + first, step), :] - p
        r[pl.ds(n + first, step), :] = x
        rh[at, :], rl[at, :] = split(x)

    def lower(first, at, p):
        to = pl.ds(n + first, step)
        yh[to, :], yl[to, :] = split(r[to, :] + p)

    def upper(first, at, p):
        yh[at, :], yl[at, :] = split(f[at, :] - p)

    phase((g1h, g1l), (rh[pl.ds(0, n), :], rl[pl.ds(0, n), :]), inner)
    phase((lowh, lowl), (fh[...], fl[...]), residual)
    phase((g2h, g2l), (rh[pl.ds(0, n), :], rl[pl.ds(0, n), :]), lower)
    phase((vh, vl), (yh[pl.ds(n, n), :], yl[pl.ds(n, n), :]), upper)


def chain_part(g1, v, low, g2, rows):
    n = g1[0].shape[0]
    width = rows[0].shape[1]
    return pl.pallas_call(
        chain_kernel,
        out_shape=(half(2 * n, width),) * 2,
        in_specs=[VMEM] * (8 + len(rows)),
        out_specs=(VMEM,) * 2,
        scratch_shapes=[pltpu.VMEM((2 * n, width), F32)]
        + [pltpu.VMEM((2 * n, width), BF16)] * 2
        + [pltpu.VMEM((n, width), F32)]
        + [pltpu.VMEM((n, width), BF16)] * 2,
        cost_estimate=pl.CostEstimate(flops=24 * n * n * width, bytes_accessed=16 * n * (n + width), transcendentals=0),
        compiler_params=pltpu.CompilerParams(vmem_limit_bytes=16 << 20),
        name="chain_part",
    )(*g1, *v, *low, *g2, *rows)


def position():
    me = lax.axis_index("col")
    return me // CORES, me % CORES


def at_end():
    chip, _ = position()
    return (chip == 0) | (chip == len(HOP_LAST) - 1)


def entry(table, index):
    value = jnp.int32(table[0])
    for i, x in enumerate(table[1:], 1):
        value = jnp.where(index == i, x, value)
    return value


def times(table, own, other, yh, yl):
    chip, core = position()
    tall = CORES * own.shape[1]
    at = pl.ds(pl.multiple_of(entry(table, chip) * tall, tall), tall)
    both = jnp.concatenate([jnp.where(core == 0, own, other), jnp.where(core == 0, other, own)], axis=1)
    return dot3(split(both), (yh[at, :], yl[at, :]))


def chosen(middle, end):
    return jnp.where(at_end(), end, middle)


def narrow(shard, other, yh, yl):
    chip, core = position()
    wide = shard.shape[1]
    at = pl.ds(pl.multiple_of(entry(HOP_LAST, chip) * CORES * wide + (core ^ other) * wide, wide), wide)
    return dot3(split(shard), (yh[at, :], yl[at, :]))


def update_kernel(tables, trail, yh, yl, *refs):
    (*pieces, middle, head), out = refs[:-1], refs[-1]
    rows = pl.ds(0, head.shape[0])
    total = trail[...]
    for i, table in enumerate(tables):
        total = total - times(table, pieces[2 * i][...], pieces[2 * i + 1][...], yh, yl)
    out[...] = total
    out[rows, :] = out[rows, :] - narrow(chosen(middle[rows, :], head[...]), 0, yh, yl)


def update_part(tables, trail, y, pieces):
    m, width = trail.shape
    wide = pieces[0].shape[1]
    return pl.pallas_call(
        functools.partial(update_kernel, tables),
        out_shape=jax.ShapeDtypeStruct((m, width), F32),
        in_specs=[VMEM] * (3 + len(pieces)),
        out_specs=VMEM,
        cost_estimate=pl.CostEstimate(
            flops=6 * m * width * wide * len(pieces), bytes_accessed=4 * m * (2 * width + wide * len(pieces)), transcendentals=0
        ),
        compiler_params=pltpu.CompilerParams(vmem_limit_bytes=16 << 20),
        name="update_part",
    )(trail, *y, *pieces)


def last_kernel(blocks, part, yh, yl, middle, middle_other, head_other, tails, out, total, sems):
    rows = head_other.shape[0]
    copies = []
    for i, (first, size) in enumerate(blocks):
        at = pl.ds(first, size)
        if first < rows:
            x = narrow(chosen(middle_other[at, :], head_other[at, :]), 1, yh, yl)
        else:
            x = times(HOP_LAST, chosen(middle[at, :], tails[:TAIL, :]), chosen(middle_other[at, :], tails[TAIL:, :]), yh, yl)
        total[at, :] = part[at, :] - x
        copies.append(pltpu.make_async_copy(total.at[at, :], out.at[at, :], sems.at[i]))
        copies[-1].start()
    for copy in copies:
        copy.wait()


def last_part(part, y, *pieces):
    m, width = part.shape
    rows, wide = pieces[2].shape
    cuts = list(range(0, rows, CHUNK // 2)) + [rows, m]
    blocks = [(first, end - first) for first, end in zip(cuts, cuts[1:])]
    return pl.pallas_call(
        functools.partial(last_kernel, blocks),
        out_shape=jax.ShapeDtypeStruct((m, width), F32),
        in_specs=[VMEM] * 7,
        out_specs=pl.BlockSpec(memory_space=pltpu.HBM),
        scratch_shapes=[pltpu.VMEM((m, width), F32), pltpu.SemaphoreType.DMA((len(blocks),))],
        cost_estimate=pl.CostEstimate(flops=6 * m * width * wide, bytes_accessed=4 * m * (2 * width + 2 * wide), transcendentals=0),
        compiler_params=pltpu.CompilerParams(vmem_limit_bytes=8 << 20),
        name="last_part",
    )(part, *y, *pieces)


def local(n_row, pivot, col_panel, row_panel, trailing):
    chips = tuple(range(len(HOP_ONE)))

    def send(x, pairs):
        idle = set(chips) - {a for a, _ in pairs}
        hops = [(CORES * a + c, CORES * b + c) for a, b in pairs for c in range(CORES)]
        swaps = [(CORES * a + c, CORES * a + (c ^ 1)) for a in sorted(idle) for c in range(CORES)]
        return lax.ppermute(x, "col", hops + swaps)

    def exchange(x):
        return send(x, ())

    def row(s):
        return lax.ppermute(row_panel, "row", [(i, i ^ s) for i in range(n_row)])

    one = send(col_panel, SEND_ONE)
    two = send(col_panel, SEND_TWO)
    middle = send(col_panel, SEND_MIDDLE)
    rows = [row_panel] + [row(s) for s in range(1, n_row)]
    one_other = exchange(one)
    *g1, u, l, d = first_part(pivot)
    vh, vl, lowh, lowl, *e, head = second_part(g1, u, l, d, one)
    head = send(head, SEND_ENDS)
    *g2, tails = third_part(e, one, one_other)
    tails = send(tails, SEND_ENDS)
    y = chain_part(g1, (vh, vl), (lowh, lowl), g2, rows)
    pieces = [col_panel, exchange(col_panel), one, one_other, two, exchange(two)]
    part = update_part((chips, HOP_ONE, HOP_TWO), trailing, y, pieces + [middle, head])
    others = exchange(middle), exchange(head)
    return last_part(part, y, middle, *others, tails)


def exact(left, right):
    return jnp.dot(left, right, precision=lax.Precision.HIGHEST, preferred_element_type=F32)


def newton_inverse(matrix):
    identity = jnp.eye(matrix.shape[0], dtype=F32)
    initial = 2.0 * identity - matrix
    return exact(initial, 2.0 * identity - exact(matrix, initial))


def gathered(pivot, col_panel, row_panel, trailing):
    cols = lax.all_gather(col_panel, "col", axis=1, tiled=True)
    rows = lax.all_gather(row_panel, "row", axis=0, tiled=True)
    n = pivot.shape[0] // 2
    top_left, top_right, low_left, low_right = pivot[:n, :n], pivot[:n, n:], pivot[n:, :n], pivot[n:, n:]
    inverse_one = newton_inverse(top_left)
    multiplier = exact(low_left, inverse_one)
    inverse_two = newton_inverse(low_right - exact(multiplier, top_right))
    factor_one = exact(cols[:, :n], inverse_one)
    factor_two = exact(cols[:, n:] - exact(factor_one, top_right), inverse_two)
    rows_two = rows[n:] - exact(multiplier, rows[:n])
    return trailing - exact(factor_one, rows[:n]) - exact(factor_two, rows_two)


def power_of_two(n):
    return n & (n - 1) == 0


def solution(mesh):
    n_row, n_col = mesh.shape["row"], mesh.shape["col"]
    line = n_col == CORES * len(HOP_ONE) and power_of_two(n_row)

    def body(pivot, col_panel, row_panel, trailing):
        if line:
            return local(n_row, pivot, col_panel, row_panel, trailing)
        return gathered(pivot, col_panel, row_panel, trailing)

    return jax.shard_map(
        body,
        mesh=mesh,
        in_specs=(P(), P("row", "col"), P("row", "col"), P("row", "col")),
        out_specs=P("row", "col"),
        check_vma=False,
    )
```

```python
import functools

import jax
import jax.numpy as jnp
from jax import lax
from jax.experimental import pallas as pl
from jax.experimental.pallas import tpu as pltpu
from jax.sharding import PartitionSpec as P


F32, BF16 = jnp.float32, jnp.bfloat16
VMEM = pl.BlockSpec(memory_space=pltpu.VMEM)
CHUNK, TAIL = 256, 64
CORES = 2
HOP_ONE, HOP_TWO, HOP_LAST = (1, 3, 0, 2), (2, 0, 3, 1), (3, 2, 1, 0)
SEND_ONE = ((1, 0), (3, 1), (0, 2), (2, 3))
SEND_TWO = ((2, 0), (0, 1), (3, 2), (1, 3))
SEND_ENDS = ((1, 0), (2, 3), (0, 1), (3, 2))
SEND_MIDDLE = ((1, 2), (2, 1))


def split(x):
    high = x.astype(BF16)
    return high, (x - high.astype(F32)).astype(BF16)


def dot(left, right):
    return jnp.dot(left, right, preferred_element_type=F32)


def dot3(left, right):
    (lh, ll), (rh, rl) = left, right
    return dot(lh, rh) + dot(lh, rl) + dot(ll, rh)


def eye(rows, cols, first):
    row = lax.broadcasted_iota(jnp.int32, (rows, cols), 0)
    col = lax.broadcasted_iota(jnp.int32, (rows, cols), 1)
    return jnp.where(row == col + first, 1.0, 0.0).astype(F32)


def each(n, body, skip=0, stop=None):
    step = min(256, n)
    for first in list(range(0, n, step))[skip:stop]:
        body(pl.ds(first, step), first)


def put(pair, cols, x):
    pair[0][:, cols], pair[1][:, cols] = split(x)


def product(left, right, cols):
    return dot3((left[0][...], left[1][...]), (right[0][:, cols], right[1][:, cols]))


def squares(n, x, e, f, **part):
    def square(cols, _):
        y = product(e, e, cols)
        put(f, cols, y)
        x[:, cols] = x[:, cols] + y

    each(n, square, **part)


def cubes(n, x, e, f, g):
    each(n, lambda cols, _: put(g, cols, x[:, cols] + product(e, f, cols)))


def quadrant(n, i, j):
    return pl.ds(i * n, n), pl.ds(j * n, n)


def first_kernel(pivot, g1h, g1l, u, l, d, a, eh, el, fh, fl, sems):
    n = a.shape[0]
    copies = [
        pltpu.make_async_copy(pivot.at[quadrant(n, i, j)], block, sems.at[2 * i + j])
        for i, j, block in ((0, 0, a), (0, 1, u), (1, 0, l), (1, 1, d))
    ]
    for copy in copies:
        copy.start()
    copies[0].wait()

    def residual(cols, first):
        x = eye(n, cols.size, first) - a[:, cols]
        a[:, cols] = x
        put((eh, el), cols, x)

    each(n, residual)
    squares(n, a, (eh, el), (fh, fl))
    cubes(n, a, (eh, el), (fh, fl), (g1h, g1l))
    for copy in copies[1:]:
        copy.wait()


def kernel_call(body, name, outs, ins, scratch, products, limit=16, aliases={}):
    n = outs[0].shape[0]
    specs = [pl.BlockSpec(memory_space=pltpu.HBM if name == "first_part" else pltpu.VMEM)] * len(ins)
    return pl.pallas_call(
        body,
        out_shape=tuple(outs),
        in_specs=specs,
        out_specs=(VMEM,) * len(outs),
        scratch_shapes=scratch,
        input_output_aliases=aliases,
        cost_estimate=pl.CostEstimate(flops=int(6 * products * n * n * n), bytes_accessed=16 * n * n, transcendentals=0),
        compiler_params=pltpu.CompilerParams(vmem_limit_bytes=limit << 20),
    )(*ins)


def half(*shape):
    return jax.ShapeDtypeStruct(shape, BF16)


def single(*shape):
    return jax.ShapeDtypeStruct(shape, F32)


def first_part(pivot):
    n = pivot.shape[0] // 2
    outs = [half(n, n)] * 2 + [single(n, n)] * 3
    scratch = [pltpu.VMEM((n, n), F32)] + [pltpu.VMEM((n, n), BF16)] * 4 + [pltpu.SemaphoreType.DMA((4,))]
    pivot = pltpu.with_memory_space_constraint(pivot, pltpu.HBM)
    return kernel_call(first_kernel, "first_part", outs, (pivot,), scratch, 2)


def second_kernel(g1h, g1l, u, l, d, shard, vh, vl, lowh, lowl, e, eh, el, head, uh, ul):
    n = u.shape[0]
    head[...] = shard[pl.ds(0, head.shape[0]), :]
    g1, v, low, up = (g1h, g1l), (vh, vl), (lowh, lowl), (uh, ul)
    each(n, lambda cols, _: put(up, cols, u[:, cols]))
    each(n, lambda cols, _: put(v, cols, u[:, cols] + product(g1, up, cols)))
    each(n, lambda cols, _: put(low, cols, l[:, cols]))

    def residual(cols, first):
        x = (eye(n, cols.size, first) - d[:, cols]) + product(low, v, cols)
        e[:, cols] = x
        put((eh, el), cols, x)

    each(n, residual)


def second_part(g1, u, l, d, shard):
    n = u.shape[0]
    m, wide = shard.shape
    outs = [half(n, n)] * 4 + [single(n, n)] + [half(n, n)] * 2 + [single(m - TAIL, wide)]
    return kernel_call(second_kernel, "second_part", outs, (*g1, u, l, d, shard), [pltpu.VMEM((n, n), BF16)] * 2, 2)


def third_kernel(e, eh, el, own, other, g2h, g2l, x, fh, fl, tails):
    n = e.shape[0]
    for i, shard in enumerate((own, other)):
        tails[pl.ds(i * TAIL, TAIL), :] = shard[pl.ds(shard.shape[0] - TAIL, TAIL), :]

    @pl.when(at_end())
    def _():
        x[...] = e[...]
        squares(n, x, (eh, el), (fh, fl))
        cubes(n, x, (eh, el), (fh, fl), (g2h, g2l))

    @pl.when(jnp.logical_not(at_end()))
    def _():
        x[...] = e[...]
        squares(n, x, (eh, el), (fh, fl), stop=1)


def third_part(e, own, other):
    n = e[0].shape[0]
    outs = [half(n, n)] * 2 + [single(n, n)] + [half(n, n)] * 2 + [single(2 * TAIL, own.shape[1])]
    return kernel_call(third_kernel, "third_part", outs, (*e, own, other), [], 2)


def late_kernel(eh, el, *refs):
    g2h, g2l, x, fh, fl = refs[-5:]

    @pl.when(jnp.logical_not(at_end()))
    def _():
        n = eh.shape[0]
        squares(n, x, (eh, el), (fh, fl), skip=1)
        cubes(n, x, (eh, el), (fh, fl), (g2h, g2l))


def late_part(e, work):
    n = e[0].shape[0]
    outs = [half(n, n)] * 2 + [single(n, n)] + [half(n, n)] * 2
    return kernel_call(late_kernel, "late_part", outs, (*e[1:], *work), [], 2, aliases={2 + i: i for i in range(5)})


def chain_kernel(g1h, g1l, vh, vl, lowh, lowl, g2h, g2l, *refs):
    rows, (yh, yl, r, rh, rl, f, fh, fl) = refs[:-8], refs[-8:]
    n = g1h.shape[0]
    deep = rows[0].shape[0]
    step = min(CHUNK, n)
    me = lax.axis_index("row")
    for s, piece in enumerate(rows):
        at = pl.ds(pl.multiple_of((me ^ s) * deep, deep), deep)
        x = piece[...]
        r[at, :] = x
        rh[at, :], rl[at, :] = split(x)

    def phase(left, right, finish):
        for first in range(0, n, step):
            at = pl.ds(first, step)
            finish(first, at, dot3((left[0][at, :], left[1][at, :]), right))

    def inner(first, at, p):
        x = r[at, :] + p
        f[at, :] = x
        fh[at, :], fl[at, :] = split(x)

    def residual(first, at, p):
        x = r[pl.ds(n + first, step), :] - p
        r[pl.ds(n + first, step), :] = x
        rh[at, :], rl[at, :] = split(x)

    def lower(first, at, p):
        to = pl.ds(n + first, step)
        yh[to, :], yl[to, :] = split(r[to, :] + p)

    def upper(first, at, p):
        yh[at, :], yl[at, :] = split(f[at, :] - p)

    phase((g1h, g1l), (rh[pl.ds(0, n), :], rl[pl.ds(0, n), :]), inner)
    phase((lowh, lowl), (fh[...], fl[...]), residual)
    phase((g2h, g2l), (rh[pl.ds(0, n), :], rl[pl.ds(0, n), :]), lower)
    phase((vh, vl), (yh[pl.ds(n, n), :], yl[pl.ds(n, n), :]), upper)


def chain_part(g1, v, low, g2, rows):
    n = g1[0].shape[0]
    width = rows[0].shape[1]
    return pl.pallas_call(
        chain_kernel,
        out_shape=(half(2 * n, width),) * 2,
        in_specs=[VMEM] * (8 + len(rows)),
        out_specs=(VMEM,) * 2,
        scratch_shapes=[pltpu.VMEM((2 * n, width), F32)]
        + [pltpu.VMEM((2 * n, width), BF16)] * 2
        + [pltpu.VMEM((n, width), F32)]
        + [pltpu.VMEM((n, width), BF16)] * 2,
        cost_estimate=pl.CostEstimate(flops=24 * n * n * width, bytes_accessed=16 * n * (n + width), transcendentals=0),
        compiler_params=pltpu.CompilerParams(vmem_limit_bytes=16 << 20),
        name="chain_part",
    )(*g1, *v, *low, *g2, *rows)


def position():
    me = lax.axis_index("col")
    return me // CORES, me % CORES


def at_end():
    chip, _ = position()
    return (chip == 0) | (chip == len(HOP_LAST) - 1)


def entry(table, index):
    value = jnp.int32(table[0])
    for i, x in enumerate(table[1:], 1):
        value = jnp.where(index == i, x, value)
    return value


def times(table, own, other, yh, yl):
    chip, core = position()
    tall = CORES * own.shape[1]
    at = pl.ds(pl.multiple_of(entry(table, chip) * tall, tall), tall)
    both = jnp.concatenate([jnp.where(core == 0, own, other), jnp.where(core == 0, other, own)], axis=1)
    return dot3(split(both), (yh[at, :], yl[at, :]))


def chosen(middle, end):
    return jnp.where(at_end(), end, middle)


def narrow(shard, other, yh, yl):
    chip, core = position()
    wide = shard.shape[1]
    at = pl.ds(pl.multiple_of(entry(HOP_LAST, chip) * CORES * wide + (core ^ other) * wide, wide), wide)
    return dot3(split(shard), (yh[at, :], yl[at, :]))


def update_kernel(tables, trail, yh, yl, *refs):
    (*pieces, middle, head), out = refs[:-1], refs[-1]
    rows = pl.ds(0, head.shape[0])
    total = trail[...]
    for i, table in enumerate(tables):
        total = total - times(table, pieces[2 * i][...], pieces[2 * i + 1][...], yh, yl)
    out[...] = total
    out[rows, :] = out[rows, :] - narrow(chosen(middle[rows, :], head[...]), 0, yh, yl)


def update_part(tables, trail, y, pieces):
    m, width = trail.shape
    wide = pieces[0].shape[1]
    return pl.pallas_call(
        functools.partial(update_kernel, tables),
        out_shape=jax.ShapeDtypeStruct((m, width), F32),
        in_specs=[VMEM] * (3 + len(pieces)),
        out_specs=VMEM,
        cost_estimate=pl.CostEstimate(
            flops=6 * m * width * wide * len(pieces), bytes_accessed=4 * m * (2 * width + wide * len(pieces)), transcendentals=0
        ),
        compiler_params=pltpu.CompilerParams(vmem_limit_bytes=16 << 20),
        name="update_part",
    )(trail, *y, *pieces)


def last_kernel(blocks, part, yh, yl, middle, middle_other, head_other, tails, out, total, sems):
    rows = head_other.shape[0]
    copies = []
    for i, (first, size) in enumerate(blocks):
        at = pl.ds(first, size)
        if first < rows:
            x = narrow(chosen(middle_other[at, :], head_other[at, :]), 1, yh, yl)
        else:
            x = times(HOP_LAST, chosen(middle[at, :], tails[:TAIL, :]), chosen(middle_other[at, :], tails[TAIL:, :]), yh, yl)
        total[at, :] = part[at, :] - x
        copies.append(pltpu.make_async_copy(total.at[at, :], out.at[at, :], sems.at[i]))
        copies[-1].start()
    for copy in copies:
        copy.wait()


def last_part(part, y, *pieces):
    m, width = part.shape
    rows, wide = pieces[2].shape
    cuts = list(range(0, rows, CHUNK // 2)) + [rows, m]
    blocks = [(first, end - first) for first, end in zip(cuts, cuts[1:])]
    return pl.pallas_call(
        functools.partial(last_kernel, blocks),
        out_shape=jax.ShapeDtypeStruct((m, width), F32),
        in_specs=[VMEM] * 7,
        out_specs=pl.BlockSpec(memory_space=pltpu.HBM),
        scratch_shapes=[pltpu.VMEM((m, width), F32), pltpu.SemaphoreType.DMA((len(blocks),))],
        cost_estimate=pl.CostEstimate(flops=6 * m * width * wide, bytes_accessed=4 * m * (2 * width + 2 * wide), transcendentals=0),
        compiler_params=pltpu.CompilerParams(vmem_limit_bytes=8 << 20),
        name="last_part",
    )(part, *y, *pieces)


def local(n_row, pivot, col_panel, row_panel, trailing):
    chips = tuple(range(len(HOP_ONE)))

    def send(x, pairs):
        idle = set(chips) - {a for a, _ in pairs}
        hops = [(CORES * a + c, CORES * b + c) for a, b in pairs for c in range(CORES)]
        swaps = [(CORES * a + c, CORES * a + (c ^ 1)) for a in sorted(idle) for c in range(CORES)]
        return lax.ppermute(x, "col", hops + swaps)

    def exchange(x):
        return send(x, ())

    def row(s):
        return lax.ppermute(row_panel, "row", [(i, i ^ s) for i in range(n_row)])

    one = send(col_panel, SEND_ONE)
    two = send(col_panel, SEND_TWO)
    middle = send(col_panel, SEND_MIDDLE)
    rows = [row_panel] + [row(s) for s in range(1, n_row)]
    one_other = exchange(one)
    *g1, u, l, d = first_part(pivot)
    vh, vl, lowh, lowl, *e, head = second_part(g1, u, l, d, one)
    head = send(head, SEND_ENDS)
    *work, tails = third_part(e, one, one_other)
    tails = send(tails, SEND_ENDS)
    g2 = late_part(e, work)[:2]
    y = chain_part(g1, (vh, vl), (lowh, lowl), g2, rows)
    pieces = [col_panel, exchange(col_panel), one, one_other, two, exchange(two)]
    part = update_part((chips, HOP_ONE, HOP_TWO), trailing, y, pieces + [middle, head])
    others = exchange(middle), exchange(head)
    return last_part(part, y, middle, *others, tails)


def exact(left, right):
    return jnp.dot(left, right, precision=lax.Precision.HIGHEST, preferred_element_type=F32)


def newton_inverse(matrix):
    identity = jnp.eye(matrix.shape[0], dtype=F32)
    initial = 2.0 * identity - matrix
    return exact(initial, 2.0 * identity - exact(matrix, initial))


def gathered(pivot, col_panel, row_panel, trailing):
    cols = lax.all_gather(col_panel, "col", axis=1, tiled=True)
    rows = lax.all_gather(row_panel, "row", axis=0, tiled=True)
    n = pivot.shape[0] // 2
    top_left, top_right, low_left, low_right = pivot[:n, :n], pivot[:n, n:], pivot[n:, :n], pivot[n:, n:]
    inverse_one = newton_inverse(top_left)
    multiplier = exact(low_left, inverse_one)
    inverse_two = newton_inverse(low_right - exact(multiplier, top_right))
    factor_one = exact(cols[:, :n], inverse_one)
    factor_two = exact(cols[:, n:] - exact(factor_one, top_right), inverse_two)
    rows_two = rows[n:] - exact(multiplier, rows[:n])
    return trailing - exact(factor_one, rows[:n]) - exact(factor_two, rows_two)


def power_of_two(n):
    return n & (n - 1) == 0


def solution(mesh):
    n_row, n_col = mesh.shape["row"], mesh.shape["col"]
    line = n_col == CORES * len(HOP_ONE) and power_of_two(n_row)

    def body(pivot, col_panel, row_panel, trailing):
        if line:
            return local(n_row, pivot, col_panel, row_panel, trailing)
        return gathered(pivot, col_panel, row_panel, trailing)

    return jax.shard_map(
        body,
        mesh=mesh,
        in_specs=(P(), P("row", "col"), P("row", "col"), P("row", "col")),
        out_specs=P("row", "col"),
        check_vma=False,
    )
```

```python
import functools

import jax
import jax.numpy as jnp
from jax import lax
from jax.experimental import pallas as pl
from jax.experimental.pallas import tpu as pltpu
from jax.sharding import PartitionSpec as P


F32, BF16 = jnp.float32, jnp.bfloat16
VMEM = pl.BlockSpec(memory_space=pltpu.VMEM)
CHUNK, TAIL = 256, 64
CORES = 2
HOP_ONE, HOP_TWO, HOP_LAST = (1, 3, 0, 2), (2, 0, 3, 1), (3, 2, 1, 0)
SEND_ONE = ((1, 0), (3, 1), (0, 2), (2, 3))
SEND_TWO = ((2, 0), (0, 1), (3, 2), (1, 3))
SEND_ENDS = ((1, 0), (2, 3), (0, 1), (3, 2))
SEND_MIDDLE = ((1, 2), (2, 1))


def split(x):
    high = x.astype(BF16)
    return high, (x - high.astype(F32)).astype(BF16)


def dot(left, right):
    return jnp.dot(left, right, preferred_element_type=F32)


def dot3(left, right):
    (lh, ll), (rh, rl) = left, right
    return dot(lh, rh) + dot(lh, rl) + dot(ll, rh)


def eye(rows, cols, first):
    row = lax.broadcasted_iota(jnp.int32, (rows, cols), 0)
    col = lax.broadcasted_iota(jnp.int32, (rows, cols), 1)
    return jnp.where(row == col + first, 1.0, 0.0).astype(F32)


def each(n, body, skip=0, stop=None):
    step = min(256, n)
    for first in list(range(0, n, step))[skip:stop]:
        body(pl.ds(first, step), first)


def put(pair, cols, x):
    pair[0][:, cols], pair[1][:, cols] = split(x)


def product(left, right, cols):
    return dot3((left[0][...], left[1][...]), (right[0][:, cols], right[1][:, cols]))


def squares(n, x, e, f, **part):
    def square(cols, _):
        y = product(e, e, cols)
        put(f, cols, y)
        x[:, cols] = x[:, cols] + y

    each(n, square, **part)


def cubes(n, x, e, f, g):
    each(n, lambda cols, _: put(g, cols, x[:, cols] + product(e, f, cols)))


def quadrant(n, i, j):
    return pl.ds(i * n, n), pl.ds(j * n, n)


def first_kernel(pivot, g1h, g1l, u, l, d, a, eh, el, fh, fl, sems):
    n = a.shape[0]
    copies = [
        pltpu.make_async_copy(pivot.at[quadrant(n, i, j)], block, sems.at[2 * i + j])
        for i, j, block in ((0, 0, a), (0, 1, u), (1, 0, l), (1, 1, d))
    ]
    for copy in copies:
        copy.start()
    copies[0].wait()

    def residual(cols, first):
        x = eye(n, cols.size, first) - a[:, cols]
        a[:, cols] = x
        put((eh, el), cols, x)

    each(n, residual)
    squares(n, a, (eh, el), (fh, fl))
    cubes(n, a, (eh, el), (fh, fl), (g1h, g1l))
    for copy in copies[1:]:
        copy.wait()


def kernel_call(body, name, outs, ins, scratch, products, limit=16, aliases={}):
    n = outs[0].shape[0]
    specs = [pl.BlockSpec(memory_space=pltpu.HBM if name == "first_part" else pltpu.VMEM)] * len(ins)
    return pl.pallas_call(
        body,
        out_shape=tuple(outs),
        in_specs=specs,
        out_specs=(VMEM,) * len(outs),
        scratch_shapes=scratch,
        input_output_aliases=aliases,
        cost_estimate=pl.CostEstimate(flops=int(6 * products * n * n * n), bytes_accessed=16 * n * n, transcendentals=0),
        compiler_params=pltpu.CompilerParams(vmem_limit_bytes=limit << 20),
    )(*ins)


def half(*shape):
    return jax.ShapeDtypeStruct(shape, BF16)


def single(*shape):
    return jax.ShapeDtypeStruct(shape, F32)


def first_part(pivot):
    n = pivot.shape[0] // 2
    outs = [half(n, n)] * 2 + [single(n, n)] * 3
    scratch = [pltpu.VMEM((n, n), F32)] + [pltpu.VMEM((n, n), BF16)] * 4 + [pltpu.SemaphoreType.DMA((4,))]
    pivot = pltpu.with_memory_space_constraint(pivot, pltpu.HBM)
    return kernel_call(first_kernel, "first_part", outs, (pivot,), scratch, 2)


def second_kernel(g1h, g1l, u, l, d, vh, vl, lowh, lowl, e, eh, el, uh, ul):
    n = u.shape[0]
    g1, v, low, up = (g1h, g1l), (vh, vl), (lowh, lowl), (uh, ul)
    each(n, lambda cols, _: put(up, cols, u[:, cols]))
    each(n, lambda cols, _: put(v, cols, u[:, cols] + product(g1, up, cols)))
    each(n, lambda cols, _: put(low, cols, l[:, cols]))

    def residual(cols, first):
        x = (eye(n, cols.size, first) - d[:, cols]) + product(low, v, cols)
        e[:, cols] = x
        put((eh, el), cols, x)

    each(n, residual)


def second_part(g1, u, l, d):
    n = u.shape[0]
    outs = [half(n, n)] * 4 + [single(n, n)] + [half(n, n)] * 2
    return kernel_call(second_kernel, "second_part", outs, (*g1, u, l, d), [pltpu.VMEM((n, n), BF16)] * 2, 2)


def cut_kernel(shard, head):
    head[...] = shard[pl.ds(0, head.shape[0]), :]


def cut_part(shard):
    m, wide = shard.shape
    return kernel_call(cut_kernel, "cut_part", [single(m - TAIL, wide)], (shard,), [], 0)[0]


def third_kernel(e, eh, el, own, other, g2h, g2l, x, fh, fl, tails):
    n = e.shape[0]
    for i, shard in enumerate((own, other)):
        tails[pl.ds(i * TAIL, TAIL), :] = shard[pl.ds(shard.shape[0] - TAIL, TAIL), :]

    @pl.when(at_end())
    def _():
        x[...] = e[...]
        squares(n, x, (eh, el), (fh, fl))
        cubes(n, x, (eh, el), (fh, fl), (g2h, g2l))

    @pl.when(jnp.logical_not(at_end()))
    def _():
        x[...] = e[...]
        squares(n, x, (eh, el), (fh, fl), stop=1)


def third_part(e, own, other):
    n = e[0].shape[0]
    outs = [half(n, n)] * 2 + [single(n, n)] + [half(n, n)] * 2 + [single(2 * TAIL, own.shape[1])]
    return kernel_call(third_kernel, "third_part", outs, (*e, own, other), [], 2)


def late_kernel(eh, el, *refs):
    g2h, g2l, x, fh, fl = refs[-5:]

    @pl.when(jnp.logical_not(at_end()))
    def _():
        n = eh.shape[0]
        squares(n, x, (eh, el), (fh, fl), skip=1)
        cubes(n, x, (eh, el), (fh, fl), (g2h, g2l))


def late_part(e, work):
    n = e[0].shape[0]
    outs = [half(n, n)] * 2 + [single(n, n)] + [half(n, n)] * 2
    return kernel_call(late_kernel, "late_part", outs, (*e[1:], *work), [], 2, aliases={2 + i: i for i in range(5)})


def chain_kernel(g1h, g1l, vh, vl, lowh, lowl, g2h, g2l, *refs):
    rows, (yh, yl, r, rh, rl, f, fh, fl) = refs[:-8], refs[-8:]
    n = g1h.shape[0]
    deep = rows[0].shape[0]
    step = min(CHUNK, n)
    me = lax.axis_index("row")
    for s, piece in enumerate(rows):
        at = pl.ds(pl.multiple_of((me ^ s) * deep, deep), deep)
        x = piece[...]
        r[at, :] = x
        rh[at, :], rl[at, :] = split(x)

    def phase(left, right, finish):
        for first in range(0, n, step):
            at = pl.ds(first, step)
            finish(first, at, dot3((left[0][at, :], left[1][at, :]), right))

    def inner(first, at, p):
        x = r[at, :] + p
        f[at, :] = x
        fh[at, :], fl[at, :] = split(x)

    def residual(first, at, p):
        x = r[pl.ds(n + first, step), :] - p
        r[pl.ds(n + first, step), :] = x
        rh[at, :], rl[at, :] = split(x)

    def lower(first, at, p):
        to = pl.ds(n + first, step)
        yh[to, :], yl[to, :] = split(r[to, :] + p)

    def upper(first, at, p):
        yh[at, :], yl[at, :] = split(f[at, :] - p)

    phase((g1h, g1l), (rh[pl.ds(0, n), :], rl[pl.ds(0, n), :]), inner)
    phase((lowh, lowl), (fh[...], fl[...]), residual)
    phase((g2h, g2l), (rh[pl.ds(0, n), :], rl[pl.ds(0, n), :]), lower)
    phase((vh, vl), (yh[pl.ds(n, n), :], yl[pl.ds(n, n), :]), upper)


def chain_part(g1, v, low, g2, rows):
    n = g1[0].shape[0]
    width = rows[0].shape[1]
    return pl.pallas_call(
        chain_kernel,
        out_shape=(half(2 * n, width),) * 2,
        in_specs=[VMEM] * (8 + len(rows)),
        out_specs=(VMEM,) * 2,
        scratch_shapes=[pltpu.VMEM((2 * n, width), F32)]
        + [pltpu.VMEM((2 * n, width), BF16)] * 2
        + [pltpu.VMEM((n, width), F32)]
        + [pltpu.VMEM((n, width), BF16)] * 2,
        cost_estimate=pl.CostEstimate(flops=24 * n * n * width, bytes_accessed=16 * n * (n + width), transcendentals=0),
        compiler_params=pltpu.CompilerParams(vmem_limit_bytes=16 << 20),
        name="chain_part",
    )(*g1, *v, *low, *g2, *rows)


def position():
    me = lax.axis_index("col")
    return me // CORES, me % CORES


def at_end():
    chip, _ = position()
    return (chip == 0) | (chip == len(HOP_LAST) - 1)


def entry(table, index):
    value = jnp.int32(table[0])
    for i, x in enumerate(table[1:], 1):
        value = jnp.where(index == i, x, value)
    return value


def times(table, own, other, yh, yl):
    chip, core = position()
    tall = CORES * own.shape[1]
    at = pl.ds(pl.multiple_of(entry(table, chip) * tall, tall), tall)
    both = jnp.concatenate([jnp.where(core == 0, own, other), jnp.where(core == 0, other, own)], axis=1)
    return dot3(split(both), (yh[at, :], yl[at, :]))


def chosen(middle, end):
    return jnp.where(at_end(), end, middle)


def narrow(shard, other, yh, yl):
    chip, core = position()
    wide = shard.shape[1]
    at = pl.ds(pl.multiple_of(entry(HOP_LAST, chip) * CORES * wide + (core ^ other) * wide, wide), wide)
    return dot3(split(shard), (yh[at, :], yl[at, :]))


def update_kernel(tables, trail, yh, yl, *refs):
    (*pieces, middle, head), out = refs[:-1], refs[-1]
    rows = pl.ds(0, head.shape[0])
    total = trail[...]
    for i, table in enumerate(tables):
        total = total - times(table, pieces[2 * i][...], pieces[2 * i + 1][...], yh, yl)
    out[...] = total
    out[rows, :] = out[rows, :] - narrow(chosen(middle[rows, :], head[...]), 0, yh, yl)


def update_part(tables, trail, y, pieces):
    m, width = trail.shape
    wide = pieces[0].shape[1]
    return pl.pallas_call(
        functools.partial(update_kernel, tables),
        out_shape=jax.ShapeDtypeStruct((m, width), F32),
        in_specs=[VMEM] * (3 + len(pieces)),
        out_specs=VMEM,
        cost_estimate=pl.CostEstimate(
            flops=6 * m * width * wide * len(pieces), bytes_accessed=4 * m * (2 * width + wide * len(pieces)), transcendentals=0
        ),
        compiler_params=pltpu.CompilerParams(vmem_limit_bytes=16 << 20),
        name="update_part",
    )(trail, *y, *pieces)


def last_kernel(blocks, part, yh, yl, middle, middle_other, head_other, tails, out, total, sems):
    rows = head_other.shape[0]
    copies = []
    for i, (first, size) in enumerate(blocks):
        at = pl.ds(first, size)
        if first < rows:
            x = narrow(chosen(middle_other[at, :], head_other[at, :]), 1, yh, yl)
        else:
            x = times(HOP_LAST, chosen(middle[at, :], tails[:TAIL, :]), chosen(middle_other[at, :], tails[TAIL:, :]), yh, yl)
        total[at, :] = part[at, :] - x
        copies.append(pltpu.make_async_copy(total.at[at, :], out.at[at, :], sems.at[i]))
        copies[-1].start()
    for copy in copies:
        copy.wait()


def last_part(part, y, *pieces):
    m, width = part.shape
    rows, wide = pieces[2].shape
    cuts = list(range(0, rows, CHUNK // 2)) + [rows, m]
    blocks = [(first, end - first) for first, end in zip(cuts, cuts[1:])]
    return pl.pallas_call(
        functools.partial(last_kernel, blocks),
        out_shape=jax.ShapeDtypeStruct((m, width), F32),
        in_specs=[VMEM] * 7,
        out_specs=pl.BlockSpec(memory_space=pltpu.HBM),
        scratch_shapes=[pltpu.VMEM((m, width), F32), pltpu.SemaphoreType.DMA((len(blocks),))],
        cost_estimate=pl.CostEstimate(flops=6 * m * width * wide, bytes_accessed=4 * m * (2 * width + 2 * wide), transcendentals=0),
        compiler_params=pltpu.CompilerParams(vmem_limit_bytes=8 << 20),
        name="last_part",
    )(part, *y, *pieces)


def local(n_row, pivot, col_panel, row_panel, trailing):
    chips = tuple(range(len(HOP_ONE)))

    def send(x, pairs):
        idle = set(chips) - {a for a, _ in pairs}
        hops = [(CORES * a + c, CORES * b + c) for a, b in pairs for c in range(CORES)]
        swaps = [(CORES * a + c, CORES * a + (c ^ 1)) for a in sorted(idle) for c in range(CORES)]
        return lax.ppermute(x, "col", hops + swaps)

    def exchange(x):
        return send(x, ())

    def row(s):
        return lax.ppermute(row_panel, "row", [(i, i ^ s) for i in range(n_row)])

    one = send(col_panel, SEND_ONE)
    two = send(col_panel, SEND_TWO)
    middle = send(col_panel, SEND_MIDDLE)
    rows = [row_panel] + [row(s) for s in range(1, n_row)]
    one_other = exchange(one)
    *g1, u, l, d = first_part(pivot)
    vh, vl, lowh, lowl, *e = second_part(g1, u, l, d)
    head = cut_part(one)
    head = send(head, SEND_ENDS)
    *work, tails = third_part(e, one, one_other)
    tails = send(tails, SEND_ENDS)
    g2 = late_part(e, work)[:2]
    y = chain_part(g1, (vh, vl), (lowh, lowl), g2, rows)
    pieces = [col_panel, exchange(col_panel), one, one_other, two, exchange(two)]
    part = update_part((chips, HOP_ONE, HOP_TWO), trailing, y, pieces + [middle, head])
    others = exchange(middle), exchange(head)
    return last_part(part, y, middle, *others, tails)


def exact(left, right):
    return jnp.dot(left, right, precision=lax.Precision.HIGHEST, preferred_element_type=F32)


def newton_inverse(matrix):
    identity = jnp.eye(matrix.shape[0], dtype=F32)
    initial = 2.0 * identity - matrix
    return exact(initial, 2.0 * identity - exact(matrix, initial))


def gathered(pivot, col_panel, row_panel, trailing):
    cols = lax.all_gather(col_panel, "col", axis=1, tiled=True)
    rows = lax.all_gather(row_panel, "row", axis=0, tiled=True)
    n = pivot.shape[0] // 2
    top_left, top_right, low_left, low_right = pivot[:n, :n], pivot[:n, n:], pivot[n:, :n], pivot[n:, n:]
    inverse_one = newton_inverse(top_left)
    multiplier = exact(low_left, inverse_one)
    inverse_two = newton_inverse(low_right - exact(multiplier, top_right))
    factor_one = exact(cols[:, :n], inverse_one)
    factor_two = exact(cols[:, n:] - exact(factor_one, top_right), inverse_two)
    rows_two = rows[n:] - exact(multiplier, rows[:n])
    return trailing - exact(factor_one, rows[:n]) - exact(factor_two, rows_two)


def power_of_two(n):
    return n & (n - 1) == 0


def solution(mesh):
    n_row, n_col = mesh.shape["row"], mesh.shape["col"]
    line = n_col == CORES * len(HOP_ONE) and power_of_two(n_row)

    def body(pivot, col_panel, row_panel, trailing):
        if line:
            return local(n_row, pivot, col_panel, row_panel, trailing)
        return gathered(pivot, col_panel, row_panel, trailing)

    return jax.shard_map(
        body,
        mesh=mesh,
        in_specs=(P(), P("row", "col"), P("row", "col"), P("row", "col")),
        out_specs=P("row", "col"),
        check_vma=False,
    )
```
